32 devices in a mesh: groups: 2 (over y), seq: 4 (over z), rows: 2 (over x), cfg: 2 (over core).
Axes of the slice: x: 2, y: 2, z: 4, core: 2. Of those that a mesh axis runs over, the one named last changes fastest.
Arguments:
- hidden: bfloat16 [2, 4096, 5120], P('cfg', ('groups', 'seq', 'rows')), parts along dimension 1, may hold values from -500 to 500
- token_order: int32 [4096], P(('groups', 'seq', 'rows')), parts along dimension 0, may hold values from 0 to 2047, as said below
- noisy_latent: float32 [16, 8, 2048], P(('groups', 'seq'), ('rows', 'cfg')), parts along dimension 0, may hold values from -6 to 6
- head_weight: bfloat16 [5120, 64], replicated, may hold values from -0.078125 to 0.078125
- head_mod: float32 [2, 5120], replicated, may hold values from -2.5 to 2.5
- guidance: float32 [1], replicated, may hold values from 3 to 7
- timestep_index: int32 [1], replicated, may hold values from 0 to 7
- step_table: int32 [9], replicated, may hold values from 0 to 1000, as said below
- vae_mean: float32 [16], replicated, may hold values from -2.5 to 2.5
- vae_std: float32 [16], replicated, may hold values from 1.1 to 3.3
- conv2_weight: float32 [16, 16], replicated, may hold values from -1.5 to 1.5
- conv2_bias: float32 [16], replicated, may hold values from -2.5 to 2.5
- conv1_weight: bfloat16 [27, 16, 384], replicated, may hold values from -0.3125 to 0.3125
- conv1_bias: float32 [384], replicated, may hold values from -2.5 to 2.5
Outputs:
- decoded: bfloat16 [16, 8, 128, 384], P(('groups', 'seq'), ('rows', 'cfg')), parts along dimension 0
The draws below stay inside these ranges and needn't reach their ends.
There are 2 independent parts, one for each index of `groups`. The reference program is written for one: setup_inputs(seed, part) draws one part's arguments, and reference() takes and returns one part's arrays. A program takes and returns all parts, laid end to end along the dimension named above; an argument that names none is the same for every part. Nothing has to cross between parts.
Inputs may be any that keep to these rules, and one draw needn't show every extreme that they name: `token_order`: a permutation of the 2048 cells, cell f * 4 * 64 + i * 64 + j being token column j of token row i of frame f; positions k * 256 to (k + 1) * 256 - 1 with k = s * 2 + r hold exactly the cells of frames s * 2 to (s + 1) * 2 - 1 and token rows r * 2 to (r + 1) * 2 - 1. `step_table`: strictly decreasing from 1000 to 0; consecutive entries differ by 90 or more.
All inputs are finite; a program needn't handle non-finite values.
Results may differ from the reference program's by a relative error of at most 0.0053.
Values may be sent and summed in bfloat16 or wider, within the bound.
No kernel may reach another device: no remote copies, remote signals or barrier semaphores. Data moves between devices by JAX's collectives and lax.ppermute only.
A program may use at most 64 MiB of HBM per device.

```python
import math
import jax
import jax.numpy as jnp
from jax import lax

D = 5120
LAT_C = 16
VAE_CH = 384
PATCH_OUT = 64
FR_DEV = 2
TR_DEV = 2
WT = 64
STEPS = 8
TOK_DEV = 256
FR = 8
HT = 4
TOKENS = 2048
LH = 8
LW = 128


def draw_hidden(key, part):
    key_base, key_rows, key_cols = jax.random.split(key, 3)
    full_shape = (2, TOKENS, D)
    row_scale = jnp.exp(jax.random.uniform(key_rows, (2, TOKENS, 1), jnp.float32) * math.log(10.0))
    col_scale = jnp.exp(jax.random.uniform(key_cols, (1, 1, D), jnp.float32) * math.log(10.0))
    base_values = jnp.clip(jax.random.normal(key_base, full_shape, jnp.float32), -5.0, 5.0)
    return (base_values * row_scale * col_scale).astype(jnp.bfloat16)


def draw_token_order(key, part):
    block_count = TOKENS // TOK_DEV
    block_keys = jax.random.split(jax.random.fold_in(key, 17), block_count)
    orders = jax.vmap(lambda block_key: jax.random.permutation(block_key, TOK_DEV))(block_keys)
    per_frame = HT // TR_DEV
    block_ids = jnp.arange(block_count, dtype=jnp.int32)[:, None]
    seq_block = block_ids // per_frame
    row_block = block_ids % per_frame
    frame_local = orders // (TR_DEV * WT)
    row_local = orders // WT % TR_DEV
    col_local = orders % WT
    cell_ids = (seq_block * FR_DEV + frame_local) * HT * WT + (row_block * TR_DEV + row_local) * WT + col_local
    return cell_ids.reshape(TOKENS).astype(jnp.int32)


def draw_step_table(key, part):
    step_gaps = jax.random.randint(jax.random.fold_in(key, 29), (STEPS - 1,), 90, 131)
    positions = 1000 - jnp.concatenate([jnp.zeros((1,), jnp.int32), jnp.cumsum(step_gaps).astype(jnp.int32)])
    return jnp.concatenate([positions, jnp.zeros((1,), jnp.int32)]).astype(jnp.int32)


def shard_levels(key, dims, cuts, smallest, top_value):
    factor_of, own = 1.0, jax.random.fold_in(key, 6)
    for position, parts in cuts:
        steps = jnp.exp(jax.random.uniform(jax.random.fold_in(own, position), (parts,), jnp.float32, smallest / len(cuts), top_value / len(cuts)))
        factor_of = factor_of * jnp.repeat(steps, dims[position] // parts).reshape([-1 if axis == position else 1 for axis in range(len(dims))])
    return factor_of


def gaussian(key, dims, scale, reach, shards=(), kind=jnp.bfloat16):
    drawn = jax.random.normal(key, dims, jnp.float32) * scale
    if len(shards) > 0:
        drawn = shard_levels(key, dims, shards, -0.22, 0.18) * drawn
    return jnp.clip(drawn, min=-reach, max=reach).astype(kind)


def setup_inputs(seed: int = 0, part: int = 0) -> dict:
    key_of = jax.random.split(jax.random.key(seed), 15)
    part_splits = jax.random.split(jax.random.fold_in(key_of[14], part), 15)
    return {
        "hidden": draw_hidden(jax.random.fold_in(jax.random.fold_in(key_of[14], part), 71), part),
        "token_order": draw_token_order(jax.random.fold_in(jax.random.fold_in(key_of[14], part), 71), part),
        "noisy_latent": gaussian(part_splits[2], (FR, LH, LW * LAT_C), 1.0, 6.0, ((0, 4), (1, 4)), jnp.float32),
        "head_weight": gaussian(key_of[3], (D, PATCH_OUT), D ** -0.5, 0.078125),
        "head_mod": gaussian(key_of[4], (2, D), 0.5, 2.5, (), jnp.float32),
        "guidance": jnp.clip(jax.random.uniform(key_of[5], (1,), jnp.float32, 3.0, 7.0), 3.0, 7.0),
        "timestep_index": jax.random.randint(key_of[6], (1,), 0, STEPS).astype(jnp.int32),
        "step_table": draw_step_table(jax.random.fold_in(key_of[14], 71), part),
        "vae_mean": gaussian(key_of[8], (LAT_C,), 0.5, 2.5, (), jnp.float32),
        "vae_std": jnp.clip(jnp.exp(jax.random.uniform(key_of[9], (LAT_C,), jnp.float32, math.log(1.1), math.log(3.3))), 1.1, 3.3),
        "conv2_weight": gaussian(key_of[10], (LAT_C, LAT_C), LAT_C ** -0.5, 1.5, (), jnp.float32),
        "conv2_bias": gaussian(key_of[11], (LAT_C,), 0.5, 2.5, (), jnp.float32),
        "conv1_weight": gaussian(key_of[12], (27, LAT_C, VAE_CH), (27 * LAT_C) ** -0.5, 0.3125),
        "conv1_bias": gaussian(key_of[13], (VAE_CH,), 0.5, 2.5, (), jnp.float32),
    }


def head_rows(row_block, head_weight, head_mod):
    values = row_block.astype(jnp.float32)
    center = lax.optimization_barrier(jnp.mean(values, axis=-1, keepdims=True))
    spread = lax.optimization_barrier(jnp.mean(jnp.square(values - center), axis=-1, keepdims=True))
    normed = (values - center) * lax.rsqrt(spread + 1e-06)
    head_in = (normed * (1.0 + head_mod[1]) + head_mod[0]).astype(jnp.bfloat16)
    return jnp.dot(head_in, head_weight, preferred_element_type=jnp.float32)

def conv_taps(padded, frames, row_count, col_count):
    pieces = []
    for step_time in range(3):
        for step_row in range(3):
            for step_col in range(3):
                pieces.append(padded[step_time:step_time + frames, step_row:step_row + row_count, step_col:step_col + col_count, :])
    return jnp.concatenate(pieces, axis=-1)

def reference(hidden, token_order, noisy_latent, head_weight, head_mod, guidance, timestep_index, step_table, vae_mean, vae_std, conv2_weight, conv2_bias, conv1_weight, conv1_bias):

    def one_block(block_index):
        row_block = lax.dynamic_slice_in_dim(hidden, block_index * TOK_DEV, TOK_DEV, 1)
        result = head_rows(row_block.reshape(2 * TOK_DEV, D), head_weight, head_mod).reshape(2, TOK_DEV, PATCH_OUT)
        return result[1] + guidance[0] * (result[0] - result[1])
    velocity = lax.map(one_block, jnp.arange(TOKENS // TOK_DEV, dtype=jnp.int32)).reshape(TOKENS, PATCH_OUT)
    cell_values = jnp.zeros((TOKENS, PATCH_OUT), jnp.float32).at[token_order].set(velocity)
    latent_velocity = cell_values.reshape(FR, HT, WT, 2, 2, LAT_C).transpose(0, 1, 3, 2, 4, 5).reshape(FR, LH, LW * LAT_C)
    step_index = timestep_index[0]
    sigma_now = step_table[step_index].astype(jnp.float32) / 1000.0
    sigma_next = step_table[step_index + 1].astype(jnp.float32) / 1000.0
    stepped = noisy_latent + (sigma_next - sigma_now) * latent_velocity
    channels = stepped.reshape(FR, LH, LW, LAT_C) * vae_std + vae_mean
    mixed_lat = jnp.einsum('fyxc,cd->fyxd', channels, conv2_weight, precision=lax.Precision.HIGHEST) + conv2_bias
    latent_in = mixed_lat.astype(jnp.bfloat16)
    padded = jnp.pad(latent_in, ((2, 0), (1, 1), (1, 1), (0, 0)))
    kernel = conv1_weight.reshape(27 * LAT_C, VAE_CH)

    def one_frame(frame_index):
        window = lax.dynamic_slice_in_dim(padded, frame_index, 3, 0)
        tap_columns = conv_taps(window, 1, LH, LW).reshape(LH * LW, 27 * LAT_C)
        result = jnp.dot(tap_columns, kernel, preferred_element_type=jnp.float32) + conv1_bias
        return result.astype(jnp.bfloat16).reshape(LH, LW, VAE_CH)
    return lax.map(one_frame, jnp.arange(FR, dtype=jnp.int32))
```

```python
import functools

import jax
import jax.numpy as jnp
from jax import lax
from jax.experimental import pallas as pl
from jax.experimental.pallas import tpu as pltpu
from jax.sharding import PartitionSpec as P

HIGHEST = lax.Precision.HIGHEST
F32 = jnp.float32
BF16 = jnp.bfloat16
NN = (((1,), (0,)), ((), ()))
NT = (((1,), (1,)), ((), ()))
TN = (((0,), (0,)), ((), ()))
RING = ("seq", "rows", "cfg")


def mm(left, right, dims=NN, precision=None):
    return lax.dot_general(left, right, dims, precision=precision, preferred_element_type=F32)


def iota(shape, dim):
    return lax.broadcasted_iota(jnp.int32, shape, dim)


def head_kernel(
    hid, wt, mod, tok, noisy, mean, std, w2, b2,
    out,
    x_v, w_v, mod_v, tok_v, noisy_v, mean_v, std_v, w2_v, b2_v,
    wcat_v, place_v, mask_v, square_v, pivot_v, small_sem, w_sem, x_sem,
):
    tokens, width = x_v.shape
    outs = w_v.shape[0]
    chans = w2_v.shape[0]
    frames, token_rows, row_lanes = noisy_v.shape
    cols = row_lanes // chans
    cells = 2 * tokens
    chunks = x_sem.shape[0]
    chunk = width // chunks
    pairs = [
        (tok, tok_v), (w2, w2_v), (mean, mean_v), (std, std_v), (b2, b2_v), (noisy, noisy_v),
    ]
    small = [pltpu.make_async_copy(a, b, small_sem.at[i]) for i, (a, b) in enumerate(pairs)]
    big = [pltpu.make_async_copy(mod, mod_v, w_sem.at[0]), pltpu.make_async_copy(wt, w_v, w_sem.at[1])]
    loads = []
    for k in range(chunks):
        span = pl.ds(k * chunk, chunk)
        loads.append(pltpu.make_async_copy(hid.at[:, span], x_v.at[:, span], x_sem.at[k]))
    for copy in small + big + loads:
        copy.start()
    for copy in small:
        copy.wait()

    frame_cells = lax.axis_size("rows") * token_rows * (cols // 2)
    cell = tok_v[...] - lax.axis_index("seq") * frames * frame_cells
    late = jnp.zeros_like(cell)
    for f in range(1, frames):
        late = late + (cell >= f * frame_cells).astype(jnp.int32)
    local = (
        cell - late * frame_cells - lax.axis_index("rows") * token_rows * (cols // 2)
        + late * token_rows * (cols // 2)
    )
    block = 128
    for e in range(2):
        target = 2 * local + e
        for start in range(0, cells, block):
            hit = iota((block, tokens), 0) + start == target
            place_v[pl.ds(start, block), pl.ds(e * tokens, tokens)] = jnp.where(hit, 1.0, 0.0).astype(BF16)

    lanes = 128
    reps = lanes // chans
    spread = (iota((chans, lanes), 1) % chans == iota((chans, lanes), 0)).astype(F32)
    row8 = iota((8, chans), 0)
    stacked = jnp.where(row8 == 0, std_v[...], jnp.where(row8 == 1, mean_v[...], b2_v[...]))
    tiled = mm(stacked, spread, NN, HIGHEST)
    mix = mm(w2_v[...], spread, TN, HIGHEST)
    diag = jnp.where(iota((chans, lanes), 1) == iota((chans, lanes), 0), tiled[2:3], 0.0)
    offset = jnp.sum(
        jnp.where(iota((chans, lanes), 1) < chans, mix * tiled[1:2] + diag, 0.0), axis=1, keepdims=True
    )
    mix = mix * tiled[0:1]

    own = iota((reps, lanes), 1) // chans == iota((reps, lanes), 0)
    tail = frames * token_rows * token_rows * chans
    for a in range(token_rows):
        for f in range(frames):
            for j in range(row_lanes // lanes):
                piece = noisy_v[f, a : a + 1, j * lanes : (j + 1) * lanes]
                mask_v[pl.ds(f * cols + j * reps, reps), :] = jnp.where(own, piece, 0.0)
        noise = mm(mix, mask_v[...], NT, HIGHEST) + offset
        for f in range(frames):
            at = tail + (f * token_rows + a) * chans
            out[pl.ds(at, chans), :] = noise[:, f * cols : (f + 1) * cols]

    blocks = outs // chans
    spot_o = iota((outs, outs), 0) // chans
    spot_j = iota((outs, outs), 1) // chans
    match = (spot_o % 2 == spot_j // 2) & (spot_o // 2 == spot_j % 2)
    mixer = jnp.where(match, jnp.concatenate([mix[:, :outs]] * blocks, axis=0), 0.0)

    for copy in big:
        copy.wait()
    piece = 512
    col_sum = jnp.zeros((outs, lanes), F32)
    shift_sum = jnp.zeros((outs, lanes), F32)
    for start in range(0, width, piece):
        span = pl.ds(start, piece)
        weight = w_v[:, span].astype(F32)
        scaled = weight * (1.0 + mod_v[1:2, span])
        high = scaled.astype(BF16)
        wcat_v[0:outs, span] = high
        wcat_v[outs : 2 * outs, span] = (scaled - high.astype(F32)).astype(BF16)
        shifted = weight * mod_v[0:1, span]
        for j in range(0, piece, lanes):
            col_sum = col_sum + scaled[:, j : j + lanes]
            shift_sum = shift_sum + shifted[:, j : j + lanes]
    wcat_v[2 * outs :, :] = jnp.ones((wcat_v.shape[0] - 2 * outs, width), BF16)
    col_sum = jnp.sum(col_sum, axis=1, keepdims=True)
    shift_sum = jnp.sum(shift_sum, axis=1, keepdims=True)

    group = 32
    total = jnp.zeros((wcat_v.shape[0], tokens), F32)
    for k in range(chunks):
        loads[k].wait()
        span = pl.ds(k * chunk, chunk)
        total = total + mm(wcat_v[:, span], x_v[:, span], NT)
        for g in range(0, tokens, group):
            rows = pl.ds(g, group)
            values = x_v[rows, span].astype(F32)
            if k == 0:
                pivot = jnp.sum(values[:, :lanes], axis=1, keepdims=True) * (1.0 / lanes)
                pivot = jnp.broadcast_to(pivot, (group, lanes))
                pivot_v[rows, :] = pivot
                squares = jnp.zeros((group, lanes), F32)
            else:
                pivot = pivot_v[rows, :]
                squares = square_v[rows, :]
            for j in range(0, chunk, lanes):
                gap = values[:, j : j + lanes] - pivot
                squares = squares + gap * gap
            square_v[rows, :] = squares

    square = mm(jnp.ones((8, lanes), F32), square_v[...], NT, HIGHEST)[0:1] * (1.0 / width)
    pivot = mm(jnp.ones((8, lanes), F32), pivot_v[...], NT, HIGHEST)[0:1] * (1.0 / lanes)
    center = total[2 * outs : 2 * outs + 1] * (1.0 / width)
    gap = center - pivot
    inverse = lax.rsqrt(jnp.maximum(square - gap * gap, 0.0) + 1e-06)
    head = (total[0:outs] + total[outs : 2 * outs] - center * col_sum) * inverse + shift_sum
    mixed = mm(mixer, head, NN, HIGHEST)
    side = outs // 2
    mixed = jnp.concatenate([mixed[:side], mixed[side:]], axis=1)
    high = mixed.astype(BF16)
    rest = mixed - high.astype(F32)
    middle = rest.astype(BF16)
    low = (rest - middle.astype(F32)).astype(BF16)
    placed = mm(jnp.concatenate([high, middle, low], axis=0), place_v[...], NT)
    placed = placed[:side] + placed[side : 2 * side] + placed[2 * side :]
    for f in range(frames):
        for i in range(token_rows):
            at = f * token_rows + i
            out[pl.ds(at * side, side), :] = placed[:, at * cols : (at + 1) * cols]


def head_call(hidden, token_order, noisy, head_weight, head_mod, mean, std, w2, b2):
    tokens, width = hidden.shape[1:]
    outs = head_weight.shape[1]
    chans = w2.shape[0]
    frames, rows, row_lanes = noisy.shape
    cols = row_lanes // chans
    chunks = 5
    hbm = pl.BlockSpec(memory_space=pl.ANY)
    vmem = pltpu.VMEM
    return pl.pallas_call(
        head_kernel,
        out_shape=jax.ShapeDtypeStruct((frames * rows * (rows + 1) * chans, cols), F32),
        in_specs=[hbm] * 9,
        out_specs=pl.BlockSpec(memory_space=pltpu.VMEM),
        scratch_shapes=[
            vmem((tokens, width), BF16), vmem((outs, width), BF16), vmem((2, width), F32),
            vmem((1, tokens), jnp.int32), vmem(noisy.shape, F32),
            vmem((1, chans), F32), vmem((1, chans), F32), vmem(w2.shape, F32), vmem((1, chans), F32),
            vmem((2 * outs + 16, width), BF16), vmem((2 * tokens, 2 * tokens), BF16),
            vmem((frames * cols, 128), F32), vmem((tokens, 128), F32), vmem((tokens, 128), F32),
            pltpu.SemaphoreType.DMA((6,)), pltpu.SemaphoreType.DMA((2,)), pltpu.SemaphoreType.DMA((chunks,)),
        ],
        compiler_params=limit(20),
        name="head",
    )(
        *(
            pltpu.with_memory_space_constraint(value, pltpu.HBM)
            for value in (
                hidden.reshape(tokens, width), head_weight.T, head_mod, token_order.reshape(1, -1), noisy,
                mean.reshape(1, -1), std.reshape(1, -1), w2, b2.reshape(1, -1),
            )
        )
    )


def merge_kernel(frames, token_rows, by_half, mine, theirs, guide, step, table, own, edge):
    half = lax.axis_index("cfg")
    side = own.shape[0] // (frames * token_rows)
    chans = edge.shape[0] // frames
    tail = own.shape[0]
    gaps = iota(table.shape, 1) - step[0]
    gaps = jnp.where(gaps == 1, table[...], jnp.where(gaps == 0, -table[...], 0))
    delta = jnp.sum(gaps.astype(F32), axis=1, keepdims=True) * (1.0 / 1000.0)
    cond = guide[0] * delta
    uncond = delta - cond
    left = jnp.where(half == 0, cond, uncond)
    right = jnp.where(half == 0, uncond, cond)
    lower = half == 1 if by_half else lax.axis_index("rows") == 0
    for f in range(frames):
        spot = pl.ds(tail + f * side, side)
        near, far = mine[spot, :], theirs[spot, :]
        values = []
        for i in range(token_rows):
            at = pl.ds((f * token_rows + i) * side, side)
            value = left * mine[at, :] + right * theirs[at, :] + jnp.where(half == i, near, far)
            value = value.astype(BF16)
            own[at, :] = value
            values.append(value)
        edge[pl.ds(f * chans, chans), :] = jnp.where(lower, values[-1][side - chans :], values[0][:chans])


def merge_call(mine, theirs, guidance, index, table, frames, token_rows, chans, by_half):
    tall = frames * token_rows * token_rows * chans
    cols = mine.shape[1]
    vmem = pl.BlockSpec(memory_space=pltpu.VMEM)
    smem = pl.BlockSpec(memory_space=pltpu.SMEM)
    return pl.pallas_call(
        functools.partial(merge_kernel, frames, token_rows, by_half),
        out_shape=(
            jax.ShapeDtypeStruct((tall, cols), BF16),
            jax.ShapeDtypeStruct((frames * chans, cols), BF16),
        ),
        in_specs=[vmem, vmem, smem, smem, vmem],
        out_specs=(vmem, vmem),
        compiler_params=limit(4),
        name="merge",
    )(mine, theirs, guidance, index, table.reshape(1, -1))


def limit(mebibytes):
    return pltpu.CompilerParams(vmem_limit_bytes=mebibytes * 2**20)


def widen_kernel(rows, weight, after, wide):
    taps, chans, chans_out = weight.shape
    span = rows + 2
    depth = span * chans
    for t in range(3):
        for w in range(3):
            for y in range(rows):
                for q in range(span):
                    u = q - y
                    if 0 <= u < 3:
                        value = weight[9 * t + 3 * u + w]
                    else:
                        value = jnp.zeros((chans, chans_out), BF16)
                    wide[w, pl.ds(t * depth + q * chans, chans), pl.ds(y * chans_out, chans_out)] = value


def widen_call(weight, after, rows):
    taps, chans, chans_out = weight.shape
    vmem = pl.BlockSpec(memory_space=pltpu.VMEM)
    return pl.pallas_call(
        functools.partial(widen_kernel, rows),
        out_shape=jax.ShapeDtypeStruct((3, 3 * (rows + 2) * chans, rows * chans_out), BF16),
        in_specs=[vmem, pl.BlockSpec(memory_space=pl.ANY)],
        out_specs=vmem,
        compiler_params=limit(8),
        name="widen",
    )(weight, after)


def conv_kernel(
    own, near, prev, prev_near, wide_v, bias,
    out,
    stack_v,
):
    frames, rows, cols, chans_out = out.shape
    depth = wide_v.shape[1] // 3
    chans = depth // (rows + 2)
    half = lax.axis_index("cfg")
    row = lax.axis_index("rows")
    past = lax.axis_index("seq") > 0
    inner = jnp.where(half == 0, row > 0, row < lax.axis_size("rows") - 1)
    first = half == 0
    band = 2 * rows * chans
    zero = jnp.zeros((chans, cols), BF16)
    tail = frames * band
    for f in range(2 * frames):
        if f < frames:
            at = pl.ds(f * band, band)
            base = jnp.where(first, prev_near[at, :], prev[at, :])
            base = jnp.where(past, base, jnp.zeros_like(base))
            at = pl.ds(tail + f * chans, chans)
            edge = jnp.where(first, prev_near[at, :], prev[at, :])
            edge = jnp.where(past & inner, edge, zero)
        else:
            base = own[pl.ds((f - frames) * band, band), :]
            edge = jnp.where(inner, near[pl.ds((f - frames) * chans, chans), :], zero)
        keep = (rows + 1) * chans
        stack_v[pl.ds(f * depth, depth), :] = jnp.where(
            first,
            jnp.concatenate([edge, base[:keep]], axis=0),
            jnp.concatenate([base[band - keep :], edge], axis=0),
        )
    latents = stack_v[...]
    shifted = []
    for w in range(3):
        pick = (iota((cols, cols), 0) + (w - 1) == iota((cols, cols), 1)).astype(F32).astype(BF16)
        shifted.append(mm(pick, latents, NT).astype(BF16))
    for f in range(frames):
        window = slice(f * depth, (f + 3) * depth)
        total = mm(shifted[0][:, window], wide_v[0])
        for w in range(1, 3):
            total = total + mm(shifted[w][:, window], wide_v[w])
        for y in range(rows):
            value = total[:, y * chans_out : (y + 1) * chans_out] + bias[...]
            out[f, y] = value.astype(BF16)


def conv_call(own, near, prev, prev_near, wide, bias, frames, rows):
    cols = own.shape[1]
    depth = wide.shape[1] // 3
    chans_out = wide.shape[2] // rows
    vmem = pl.BlockSpec(memory_space=pltpu.VMEM)
    return pl.pallas_call(
        conv_kernel,
        out_shape=jax.ShapeDtypeStruct((frames, rows, cols, chans_out), BF16),
        in_specs=[vmem] * 6,
        out_specs=vmem,
        scratch_shapes=[pltpu.VMEM((2 * frames * depth, cols), BF16)],
        compiler_params=limit(8),
        name="conv",
    )(own, near, prev, prev_near, wide, bias)


def routes(sizes, rule):
    seqs, rows, halves = sizes
    pairs = []
    for s in range(seqs):
        for r in range(rows):
            for c in range(halves):
                to = rule(s, r, c)
                if 0 <= to[0] < seqs and 0 <= to[1] < rows:
                    pairs.append(((s * rows + r) * halves + c, (to[0] * rows + to[1]) * halves + to[2]))
    return pairs


def send(value, sizes, rule):
    return lax.ppermute(value, RING, routes(sizes, rule))


def per_device(
    hidden,
    token_order,
    noisy_latent,
    head_weight,
    head_mod,
    guidance,
    timestep_index,
    step_table,
    vae_mean,
    vae_std,
    conv2_weight,
    conv2_bias,
    conv1_weight,
    conv1_bias,
):
    frames, rows, _ = noisy_latent.shape
    chans = conv2_weight.shape[0]
    sizes = tuple(lax.axis_size(axis) for axis in RING)
    seqs, row_count, _ = sizes
    part = head_call(
        hidden, token_order, noisy_latent, head_weight, head_mod, vae_mean, vae_std, conv2_weight, conv2_bias
    )
    other = send(part, sizes, lambda s, r, c: (s, r, 1 - c))
    own, edge = merge_call(
        part, other, guidance, timestep_index, step_table, frames, rows, chans, row_count != 2
    )
    if row_count == 2:
        top = seqs - 1

        def along(s, r, c):
            if c == 1:
                return (s + 1, r, 1) if s < top else (s, r, 0)
            return (s - 1, r, 0) if s > 0 else (s, r, 1)

        def across(s, r, c):
            if c == 1:
                return (s + 1, 1 - r, 1) if s < top else (s, 1 - r, 0)
            return (s - 1, r, 0) if s > 0 else (s, 1 - r, 1)

        prev = send(own, sizes, along)
        near = send(edge, sizes, lambda s, r, c: (s, 1 - r, c))
        prev_edge = send(edge, sizes, across)
        prev, near, prev_edge = lax.optimization_barrier((prev, near, prev_edge))
        prev = jnp.concatenate([prev, prev_edge], axis=0)
        prev_near = send(prev, sizes, lambda s, r, c: (s, r, 1 - c))
    else:
        near = send(edge, sizes, lambda s, r, c: (s, r - 1, 1) if c == 0 else (s, r + 1, 0))
        prev = send(own, sizes, lambda s, r, c: (s + 1, r, c))
        prev_edge = send(edge, sizes, lambda s, r, c: (s + 1, r - 1, 1) if c == 0 else (s + 1, r + 1, 0))
        prev = prev_near = jnp.concatenate([prev, prev_edge], axis=0)
    wide = widen_call(conv1_weight, edge, rows)
    return conv_call(own, near, prev, prev_near, wide, conv1_bias.reshape(1, -1), frames, rows)


def solution(mesh):
    return jax.shard_map(
        per_device,
        mesh=mesh,
        in_specs=(
            P("cfg", ("groups", "seq", "rows"), None),
            P(("groups", "seq", "rows")),
            P(("groups", "seq"), ("rows", "cfg"), None),
            P(),
            P(),
            P(),
            P(),
            P(),
            P(),
            P(),
            P(),
            P(),
            P(),
            P(),
        ),
        out_specs=P(("groups", "seq"), ("rows", "cfg"), None, None),
        check_vma=False,
    )
```

```python
import functools

import jax
import jax.numpy as jnp
from jax import lax
from jax.experimental import pallas as pl
from jax.experimental.pallas import tpu as pltpu
from jax.sharding import PartitionSpec as P


HIGHEST = lax.Precision.HIGHEST
F32 = jnp.float32
BF16 = jnp.bfloat16
NN = (((1,), (0,)), ((), ()))
NT = (((1,), (1,)), ((), ()))
TN = (((0,), (0,)), ((), ()))
RING = ("seq", "rows", "cfg")


def mm(left, right, dims=NN, precision=None):
    return lax.dot_general(left, right, dims, precision=precision, preferred_element_type=F32)


def iota(shape, dim):
    return lax.broadcasted_iota(jnp.int32, shape, dim)


def head_kernel(
    hid, wt, mod, tok, noisy, mean, std, w2, b2,
    out,
    x_v, w_v, mod_v, tok_v, noisy_v, mean_v, std_v, w2_v, b2_v,
    wcat_v, place_v, mask_v, square_v, pivot_v, small_sem, w_sem, x_sem,
):
    tokens, width = x_v.shape
    outs = w_v.shape[0]
    chans = w2_v.shape[0]
    frames, token_rows, row_lanes = noisy_v.shape
    cols = row_lanes // chans
    cells = 2 * tokens
    chunks = x_sem.shape[0]
    chunk = width // chunks
    pairs = [
        (tok, tok_v), (w2, w2_v), (mean, mean_v), (std, std_v), (b2, b2_v), (noisy, noisy_v),
    ]
    small = [pltpu.make_async_copy(a, b, small_sem.at[i]) for i, (a, b) in enumerate(pairs)]
    big = [pltpu.make_async_copy(mod, mod_v, w_sem.at[0]), pltpu.make_async_copy(wt, w_v, w_sem.at[1])]
    loads = []
    for k in range(chunks):
        span = pl.ds(k * chunk, chunk)
        loads.append(pltpu.make_async_copy(hid.at[:, span], x_v.at[:, span], x_sem.at[k]))
    for copy in small + big + loads[:1]:
        copy.start()
    for copy in small:
        copy.wait()

    frame_cells = lax.axis_size("rows") * token_rows * (cols // 2)
    cell = tok_v[...] - lax.axis_index("seq") * frames * frame_cells
    late = jnp.zeros_like(cell)
    for f in range(1, frames):
        late = late + (cell >= f * frame_cells).astype(jnp.int32)
    local = (
        cell - late * frame_cells - lax.axis_index("rows") * token_rows * (cols // 2)
        + late * token_rows * (cols // 2)
    )
    block = 128
    for e in range(2):
        target = 2 * local + e
        for start in range(0, cells, block):
            hit = iota((block, tokens), 0) + start == target
            place_v[pl.ds(start, block), pl.ds(e * tokens, tokens)] = jnp.where(hit, 1.0, 0.0).astype(BF16)

    lanes = 128
    reps = lanes // chans
    spread = (iota((chans, lanes), 1) % chans == iota((chans, lanes), 0)).astype(F32)
    row8 = iota((8, chans), 0)
    stacked = jnp.where(row8 == 0, std_v[...], jnp.where(row8 == 1, mean_v[...], b2_v[...]))
    tiled = mm(stacked, spread, NN, HIGHEST)
    mix = mm(w2_v[...], spread, TN, HIGHEST)
    diag = jnp.where(iota((chans, lanes), 1) == iota((chans, lanes), 0), tiled[2:3], 0.0)
    offset = jnp.sum(
        jnp.where(iota((chans, lanes), 1) < chans, mix * tiled[1:2] + diag, 0.0), axis=1, keepdims=True
    )
    mix = mix * tiled[0:1]

    own = iota((reps, lanes), 1) // chans == iota((reps, lanes), 0)
    tail = frames * token_rows * token_rows * chans
    for a in range(token_rows):
        for f in range(frames):
            for j in range(row_lanes // lanes):
                piece = noisy_v[f, a : a + 1, j * lanes : (j + 1) * lanes]
                mask_v[pl.ds(f * cols + j * reps, reps), :] = jnp.where(own, piece, 0.0)
        noise = mm(mix, mask_v[...], NT, HIGHEST) + offset
        for f in range(frames):
            at = tail + (f * token_rows + a) * chans
            out[pl.ds(at, chans), :] = noise[:, f * cols : (f + 1) * cols]

    blocks = outs // chans
    spot_o = iota((outs, outs), 0) // chans
    spot_j = iota((outs, outs), 1) // chans
    match = (spot_o % 2 == spot_j // 2) & (spot_o // 2 == spot_j % 2)
    mixer = jnp.where(match, jnp.concatenate([mix[:, :outs]] * blocks, axis=0), 0.0)

    for copy in big:
        copy.wait()
    for copy in loads[1:5]:
        copy.start()
    piece = 512
    col_sum = jnp.zeros((outs, lanes), F32)
    shift_sum = jnp.zeros((outs, lanes), F32)
    for start in range(0, width, piece):
        span = pl.ds(start, piece)
        weight = w_v[:, span].astype(F32)
        scaled = weight * (1.0 + mod_v[1:2, span])
        high = scaled.astype(BF16)
        wcat_v[0:outs, span] = high
        wcat_v[outs : 2 * outs, span] = (scaled - high.astype(F32)).astype(BF16)
        shifted = weight * mod_v[0:1, span]
        for j in range(0, piece, lanes):
            col_sum = col_sum + scaled[:, j : j + lanes]
            shift_sum = shift_sum + shifted[:, j : j + lanes]
    wcat_v[2 * outs :, :] = jnp.ones((wcat_v.shape[0] - 2 * outs, width), BF16)
    col_sum = jnp.sum(col_sum, axis=1, keepdims=True)
    shift_sum = jnp.sum(shift_sum, axis=1, keepdims=True)

    group = 32
    total = jnp.zeros((wcat_v.shape[0], tokens), F32)
    for k in range(chunks):
        loads[k].wait()
        for copy in loads[5:] if k == 0 else ():
            copy.start()
        span = pl.ds(k * chunk, chunk)
        total = total + mm(wcat_v[:, span], x_v[:, span], NT)
        for g in range(0, tokens, group):
            rows = pl.ds(g, group)
            values = x_v[rows, span].astype(F32)
            if k == 0:
                pivot = jnp.sum(values[:, :lanes], axis=1, keepdims=True) * (1.0 / lanes)
                pivot = jnp.broadcast_to(pivot, (group, lanes))
                pivot_v[rows, :] = pivot
                squares = jnp.zeros((group, lanes), F32)
            else:
                pivot = pivot_v[rows, :]
                squares = square_v[rows, :]
            for j in range(0, chunk, lanes):
                gap = values[:, j : j + lanes] - pivot
                squares = squares + gap * gap
            square_v[rows, :] = squares

    square = mm(jnp.ones((8, lanes), F32), square_v[...], NT, HIGHEST)[0:1] * (1.0 / width)
    pivot = mm(jnp.ones((8, lanes), F32), pivot_v[...], NT, HIGHEST)[0:1] * (1.0 / lanes)
    center = total[2 * outs : 2 * outs + 1] * (1.0 / width)
    gap = center - pivot
    inverse = lax.rsqrt(jnp.maximum(square - gap * gap, 0.0) + 1e-06)
    head = (total[0:outs] + total[outs : 2 * outs] - center * col_sum) * inverse + shift_sum
    mixed = mm(mixer, head, NN, HIGHEST)
    side = outs // 2
    mixed = jnp.concatenate([mixed[:side], mixed[side:]], axis=1)
    high = mixed.astype(BF16)
    rest = mixed - high.astype(F32)
    middle = rest.astype(BF16)
    low = (rest - middle.astype(F32)).astype(BF16)
    placed = mm(jnp.concatenate([high, middle, low], axis=0), place_v[...], NT)
    placed = placed[:side] + placed[side : 2 * side] + placed[2 * side :]
    for f in range(frames):
        for i in range(token_rows):
            at = f * token_rows + i
            out[pl.ds(at * side, side), :] = placed[:, at * cols : (at + 1) * cols]


def head_call(hidden, token_order, noisy, head_weight, head_mod, mean, std, w2, b2):
    tokens, width = hidden.shape[1:]
    outs = head_weight.shape[1]
    chans = w2.shape[0]
    frames, rows, row_lanes = noisy.shape
    cols = row_lanes // chans
    chunks = 5
    hbm = pl.BlockSpec(memory_space=pl.ANY)
    vmem = pltpu.VMEM
    return pl.pallas_call(
        head_kernel,
        out_shape=jax.ShapeDtypeStruct((frames * rows * (rows + 1) * chans, cols), F32),
        in_specs=[hbm] * 9,
        out_specs=pl.BlockSpec(memory_space=pltpu.VMEM),
        scratch_shapes=[
            vmem((tokens, width), BF16), vmem((outs, width), BF16), vmem((2, width), F32),
            vmem((1, tokens), jnp.int32), vmem(noisy.shape, F32),
            vmem((1, chans), F32), vmem((1, chans), F32), vmem(w2.shape, F32), vmem((1, chans), F32),
            vmem((2 * outs + 16, width), BF16), vmem((2 * tokens, 2 * tokens), BF16),
            vmem((frames * cols, 128), F32), vmem((tokens, 128), F32), vmem((tokens, 128), F32),
            pltpu.SemaphoreType.DMA((6,)), pltpu.SemaphoreType.DMA((2,)), pltpu.SemaphoreType.DMA((chunks,)),
        ],
        compiler_params=limit(20),
        name="head",
    )(
        *(
            pltpu.with_memory_space_constraint(value, pltpu.HBM)
            for value in (
                hidden.reshape(tokens, width), head_weight.T, head_mod, token_order.reshape(1, -1), noisy,
                mean.reshape(1, -1), std.reshape(1, -1), w2, b2.reshape(1, -1),
            )
        )
    )


def merge_kernel(frames, token_rows, by_half, mine, theirs, guide, step, table, own, edge):
    half = lax.axis_index("cfg")
    side = own.shape[0] // (frames * token_rows)
    chans = edge.shape[0] // frames
    tail = own.shape[0]
    gaps = iota(table.shape, 1) - step[0]
    gaps = jnp.where(gaps == 1, table[...], jnp.where(gaps == 0, -table[...], 0))
    delta = jnp.sum(gaps.astype(F32), axis=1, keepdims=True) * (1.0 / 1000.0)
    cond = guide[0] * delta
    uncond = delta - cond
    left = jnp.where(half == 0, cond, uncond)
    right = jnp.where(half == 0, uncond, cond)
    lower = half == 1 if by_half else lax.axis_index("rows") == 0
    for f in range(frames):
        spot = pl.ds(tail + f * side, side)
        near, far = mine[spot, :], theirs[spot, :]
        values = []
        for i in range(token_rows):
            at = pl.ds((f * token_rows + i) * side, side)
            value = left * mine[at, :] + right * theirs[at, :] + jnp.where(half == i, near, far)
            value = value.astype(BF16)
            own[at, :] = value
            values.append(value)
        edge[pl.ds(f * chans, chans), :] = jnp.where(lower, values[-1][side - chans :], values[0][:chans])


def merge_call(mine, theirs, guidance, index, table, frames, token_rows, chans, by_half):
    tall = frames * token_rows * token_rows * chans
    cols = mine.shape[1]
    vmem = pl.BlockSpec(memory_space=pltpu.VMEM)
    smem = pl.BlockSpec(memory_space=pltpu.SMEM)
    return pl.pallas_call(
        functools.partial(merge_kernel, frames, token_rows, by_half),
        out_shape=(
            jax.ShapeDtypeStruct((tall, cols), BF16),
            jax.ShapeDtypeStruct((frames * chans, cols), BF16),
        ),
        in_specs=[vmem, vmem, smem, smem, vmem],
        out_specs=(vmem, vmem),
        compiler_params=limit(4),
        name="merge",
    )(mine, theirs, guidance, index, table.reshape(1, -1))


def limit(mebibytes):
    return pltpu.CompilerParams(vmem_limit_bytes=mebibytes * 2**20)


def widen_kernel(rows, weight, after, wide):
    _, chans, chans_out = weight.shape
    span = rows + 2
    depth = span * chans
    for t in range(3):
        for w in range(3):
            for y in range(rows):
                for q in range(span):
                    u = q - y
                    if 0 <= u < 3:
                        value = weight[9 * t + 3 * u + w]
                    else:
                        value = jnp.zeros((chans, chans_out), BF16)
                    wide[w, pl.ds(t * depth + q * chans, chans), pl.ds(y * chans_out, chans_out)] = value


def widen_call(weight, after, rows):
    _, chans, chans_out = weight.shape
    vmem = pl.BlockSpec(memory_space=pltpu.VMEM)
    return pl.pallas_call(
        functools.partial(widen_kernel, rows),
        out_shape=jax.ShapeDtypeStruct((3, 3 * (rows + 2) * chans, rows * chans_out), BF16),
        in_specs=[vmem, pl.BlockSpec(memory_space=pl.ANY)],
        out_specs=vmem,
        compiler_params=limit(8),
        name="widen",
    )(weight, after)


def conv_kernel(
    own, near, prev, prev_near, wide_v, bias,
    result,
    stack_v, out, out_sem,
):
    frames, rows, cols, chans_out = out.shape
    stores = []
    depth = wide_v.shape[1] // 3
    chans = depth // (rows + 2)
    half = lax.axis_index("cfg")
    row = lax.axis_index("rows")
    past = lax.axis_index("seq") > 0
    inner = jnp.where(half == 0, row > 0, row < lax.axis_size("rows") - 1)
    first = half == 0
    band = 2 * rows * chans
    zero = jnp.zeros((chans, cols), BF16)
    tail = frames * band + near.shape[0]
    for f in range(2 * frames):
        if f < frames:
            at = pl.ds(f * band, band)
            base = jnp.where(first, prev_near[at, :], prev[at, :])
            base = jnp.where(past, base, jnp.zeros_like(base))
            at = pl.ds(tail + f * chans, chans)
            edge = jnp.where(first, prev_near[at, :], prev[at, :])
            edge = jnp.where(past & inner, edge, zero)
        else:
            base = own[pl.ds((f - frames) * band, band), :]
            edge = jnp.where(inner, near[pl.ds((f - frames) * chans, chans), :], zero)
        keep = (rows + 1) * chans
        stack_v[pl.ds(f * depth, depth), :] = jnp.where(
            first,
            jnp.concatenate([edge, base[:keep]], axis=0),
            jnp.concatenate([base[band - keep :], edge], axis=0),
        )
    latents = stack_v[...]
    shifted = []
    for w in range(3):
        pick = (iota((cols, cols), 0) + (w - 1) == iota((cols, cols), 1)).astype(F32).astype(BF16)
        shifted.append(mm(pick, latents, NT).astype(BF16))
    for f in range(frames):
        window = slice(f * depth, (f + 3) * depth)
        total = mm(shifted[0][:, window], wide_v[0])
        for w in range(1, 3):
            total = total + mm(shifted[w][:, window], wide_v[w])
        for y in range(rows):
            value = total[:, y * chans_out : (y + 1) * chans_out] + bias[...]
            out[f, y] = value.astype(BF16)
            stores.append(pltpu.make_async_copy(out.at[f, y], result.at[f, y], out_sem.at[f * rows + y]))
            stores[-1].start()
    for copy in stores:
        copy.wait()


def conv_call(own, near, prev, prev_near, wide, bias, frames, rows):
    cols = own.shape[1]
    depth = wide.shape[1] // 3
    chans_out = wide.shape[2] // rows
    vmem = pl.BlockSpec(memory_space=pltpu.VMEM)
    return pl.pallas_call(
        conv_kernel,
        out_shape=jax.ShapeDtypeStruct((frames, rows, cols, chans_out), BF16),
        in_specs=[vmem] * 6,
        out_specs=pl.BlockSpec(memory_space=pl.ANY),
        scratch_shapes=[
            pltpu.VMEM((2 * frames * depth, cols), BF16),
            pltpu.VMEM((frames, rows, cols, chans_out), BF16),
            pltpu.SemaphoreType.DMA((frames * rows,)),
        ],
        compiler_params=limit(8),
        name="conv",
    )(own, near, prev, prev_near, wide, bias)


def routes(sizes, rule):
    seqs, rows, halves = sizes
    pairs = []
    for s in range(seqs):
        for r in range(rows):
            for c in range(halves):
                to = rule(s, r, c)
                if 0 <= to[0] < seqs and 0 <= to[1] < rows:
                    pairs.append(((s * rows + r) * halves + c, (to[0] * rows + to[1]) * halves + to[2]))
    return pairs


def send(value, sizes, rule):
    return lax.ppermute(value, RING, routes(sizes, rule))


def per_device(
    hidden,
    token_order,
    noisy_latent,
    head_weight,
    head_mod,
    guidance,
    timestep_index,
    step_table,
    vae_mean,
    vae_std,
    conv2_weight,
    conv2_bias,
    conv1_weight,
    conv1_bias,
):
    frames, rows, _ = noisy_latent.shape
    chans = conv2_weight.shape[0]
    sizes = tuple(lax.axis_size(axis) for axis in RING)
    seqs, row_count, _ = sizes
    part = head_call(
        hidden, token_order, noisy_latent, head_weight, head_mod, vae_mean, vae_std, conv2_weight, conv2_bias
    )
    other = send(part, sizes, lambda s, r, c: (s, r, 1 - c))
    own, edge = merge_call(
        part, other, guidance, timestep_index, step_table, frames, rows, chans, row_count != 2
    )
    if row_count == 2:
        top = seqs - 1

        def along(s, r, c):
            if c == 1:
                return (s + 1, r, 1) if s < top else (s, r, 0)
            return (s - 1, r, 0) if s > 0 else (s, r, 1)

        def across(s, r, c):
            if c == 1:
                return (s + 1, 1 - r, 1) if s < top else (s, 1 - r, 0)
            return (s - 1, r, 0) if s > 0 else (s, 1 - r, 1)

        prev = send(own, sizes, along)
        near = send(edge, sizes, lambda s, r, c: (s, 1 - r, c))
        prev_edge = send(edge, sizes, across)
        prev = jnp.concatenate([prev, near, prev_edge], axis=0)
        prev_near = send(prev, sizes, lambda s, r, c: (s, r, 1 - c))
    else:
        near = send(edge, sizes, lambda s, r, c: (s, r - 1, 1) if c == 0 else (s, r + 1, 0))
        prev = send(own, sizes, lambda s, r, c: (s + 1, r, c))
        prev_edge = send(edge, sizes, lambda s, r, c: (s + 1, r - 1, 1) if c == 0 else (s + 1, r + 1, 0))
        prev = prev_near = jnp.concatenate([prev, near, prev_edge], axis=0)
    wide = widen_call(conv1_weight, edge, rows)
    return conv_call(own, near, prev, prev_near, wide, conv1_bias.reshape(1, -1), frames, rows)


def solution(mesh):
    return jax.shard_map(
        per_device,
        mesh=mesh,
        in_specs=(
            P("cfg", ("groups", "seq", "rows"), None),
            P(("groups", "seq", "rows")),
            P(("groups", "seq"), ("rows", "cfg"), None),
            P(),
            P(),
            P(),
            P(),
            P(),
            P(),
            P(),
            P(),
            P(),
            P(),
            P(),
        ),
        out_specs=P(("groups", "seq"), ("rows", "cfg"), None, None),
        check_vma=False,
    )
```

```python
import functools

import jax
import jax.numpy as jnp
from jax import lax
from jax.experimental import pallas as pl
from jax.experimental.pallas import tpu as pltpu
from jax.sharding import PartitionSpec as P


HIGHEST = lax.Precision.HIGHEST
F32 = jnp.float32
BF16 = jnp.bfloat16
NN = (((1,), (0,)), ((), ()))
NT = (((1,), (1,)), ((), ()))
TN = (((0,), (0,)), ((), ()))
RING = ("seq", "rows", "cfg")


def mm(left, right, dims=NN, precision=None):
    return lax.dot_general(left, right, dims, precision=precision, preferred_element_type=F32)


def iota(shape, dim):
    return lax.broadcasted_iota(jnp.int32, shape, dim)


def split(value, terms):
    parts = []
    for _ in range(terms):
        parts.append(value.astype(BF16))
        value = value - parts[-1].astype(F32)
    return parts


def head_kernel(
    hid, wt, mod, tok, noisy, mean, std, w2, b2,
    out,
    x_v, w_v, mod_v, tok_v, noisy_v, mean_v, std_v, w2_v, b2_v,
    wcat_v, place_v, mask_v, square_v, pivot_v, small_sem, w_sem, x_sem,
):
    tokens, width = x_v.shape
    outs = w_v.shape[0]
    chans = w2_v.shape[0]
    frames, token_rows, row_lanes = noisy_v.shape
    cols = row_lanes // chans
    cells = 2 * tokens
    chunks = x_sem.shape[0]
    chunk = width // chunks
    pairs = [
        (tok, tok_v), (w2, w2_v), (mean, mean_v), (std, std_v), (b2, b2_v), (noisy, noisy_v),
    ]
    small = [pltpu.make_async_copy(a, b, small_sem.at[i]) for i, (a, b) in enumerate(pairs)]
    big = [pltpu.make_async_copy(mod, mod_v, w_sem.at[0]), pltpu.make_async_copy(wt, w_v, w_sem.at[1])]
    loads = []
    for k in range(chunks):
        span = pl.ds(k * chunk, chunk)
        loads.append(pltpu.make_async_copy(hid.at[:, span], x_v.at[:, span], x_sem.at[k]))
    for copy in small + big + loads[:1]:
        copy.start()
    for copy in small:
        copy.wait()

    frame_cells = lax.axis_size("rows") * token_rows * (cols // 2)
    cell = tok_v[...] - lax.axis_index("seq") * frames * frame_cells
    late = jnp.zeros_like(cell)
    for f in range(1, frames):
        late = late + (cell >= f * frame_cells).astype(jnp.int32)
    local = (
        cell - late * frame_cells - lax.axis_index("rows") * token_rows * (cols // 2)
        + late * token_rows * (cols // 2)
    )
    block = 128
    for e in range(2):
        target = 2 * local + e
        for start in range(0, cells, block):
            hit = iota((block, tokens), 0) + start == target
            place_v[pl.ds(start, block), pl.ds(e * tokens, tokens)] = jnp.where(hit, 1.0, 0.0).astype(BF16)

    lanes = 128
    reps = lanes // chans
    spread = (iota((chans, lanes), 1) % chans == iota((chans, lanes), 0)).astype(F32)
    row8 = iota((8, chans), 0)
    stacked = jnp.where(row8 == 0, std_v[...], jnp.where(row8 == 1, mean_v[...], b2_v[...]))
    tiled = mm(stacked, spread, NN, HIGHEST)
    mix = mm(w2_v[...], spread, TN, HIGHEST)
    diag = jnp.where(iota((chans, lanes), 1) == iota((chans, lanes), 0), tiled[2:3], 0.0)
    offset = jnp.sum(
        jnp.where(iota((chans, lanes), 1) < chans, mix * tiled[1:2] + diag, 0.0), axis=1, keepdims=True
    )
    mix = mix * tiled[0:1]

    own = iota((reps, lanes), 1) // chans == iota((reps, lanes), 0)
    tail = frames * token_rows * token_rows * chans
    for a in range(token_rows):
        for f in range(frames):
            for j in range(row_lanes // lanes):
                piece = noisy_v[f, a : a + 1, j * lanes : (j + 1) * lanes]
                mask_v[pl.ds(f * cols + j * reps, reps), :] = jnp.where(own, piece, 0.0)
        noise = mm(mix, mask_v[...], NT, HIGHEST) + offset
        for f in range(frames):
            at = tail + (f * token_rows + a) * chans
            out[pl.ds(at, chans), :] = noise[:, f * cols : (f + 1) * cols]

    blocks = outs // chans
    spot_o = iota((outs, outs), 0) // chans
    spot_j = iota((outs, outs), 1) // chans
    match = (spot_o % 2 == spot_j // 2) & (spot_o // 2 == spot_j % 2)
    mixer = jnp.where(match, jnp.concatenate([mix[:, :outs]] * blocks, axis=0), 0.0)
    high, low = split(mixer, 2)
    mixer = jnp.concatenate([high, high, low], axis=1)

    for copy in big:
        copy.wait()
    for copy in loads[1:5]:
        copy.start()
    piece = 512
    col_sum = jnp.zeros((outs, lanes), F32)
    shift_sum = jnp.zeros((outs, lanes), F32)
    for start in range(0, width, piece):
        span = pl.ds(start, piece)
        weight = w_v[:, span].astype(F32)
        scaled = weight * (1.0 + mod_v[1:2, span])
        high = scaled.astype(BF16)
        wcat_v[0:outs, span] = high
        wcat_v[outs : 2 * outs, span] = (scaled - high.astype(F32)).astype(BF16)
        shifted = weight * mod_v[0:1, span]
        for j in range(0, piece, lanes):
            col_sum = col_sum + scaled[:, j : j + lanes]
            shift_sum = shift_sum + shifted[:, j : j + lanes]
    wcat_v[2 * outs :, :] = jnp.ones((wcat_v.shape[0] - 2 * outs, width), BF16)
    col_sum = jnp.sum(col_sum, axis=1, keepdims=True)
    shift_sum = jnp.sum(shift_sum, axis=1, keepdims=True)

    group = 32
    total = jnp.zeros((wcat_v.shape[0], tokens), F32)
    pivot_row = None
    for k in range(chunks):
        loads[k].wait()
        for copy in loads[5:] if k == 0 else ():
            copy.start()
        span = pl.ds(k * chunk, chunk)
        total = total + mm(wcat_v[:, span], x_v[:, span], NT)
        for g in range(0, tokens, group):
            rows = pl.ds(g, group)
            values = x_v[rows, span].astype(F32)
            if k == 0:
                pivot = jnp.sum(values[:, :lanes], axis=1, keepdims=True) * (1.0 / lanes)
                pivot = jnp.broadcast_to(pivot, (group, lanes))
                pivot_v[rows, :] = pivot
                squares = jnp.zeros((group, lanes), F32)
            else:
                pivot = pivot_v[rows, :]
                squares = square_v[rows, :]
            for j in range(0, chunk, lanes):
                gap = values[:, j : j + lanes] - pivot
                squares = squares + gap * gap
            square_v[rows, :] = squares
        if k == 0:
            parts = jnp.concatenate(split(pivot_v[...], 3), axis=1)
            pivot_row = mm(jnp.ones((16, 3 * lanes), BF16), parts, NT)[0:1] * (1.0 / lanes)

    parts = jnp.concatenate(split(square_v[...], 3), axis=1)
    square = mm(jnp.ones((16, 3 * lanes), BF16), parts, NT)[0:1] * (1.0 / width)
    center = total[2 * outs : 2 * outs + 1] * (1.0 / width)
    gap = center - pivot_row
    inverse = lax.rsqrt(jnp.maximum(square - gap * gap, 0.0) + 1e-06)
    head = (total[0:outs] + total[outs : 2 * outs] - center * col_sum) * inverse + shift_sum
    high, low = split(head, 2)
    mixed = mm(mixer, jnp.concatenate([high, low, high], axis=0))
    side = outs // 2
    mixed = jnp.concatenate([mixed[:side], mixed[side:]], axis=1)
    placed = mm(jnp.concatenate(split(mixed, 3), axis=0), place_v[...], NT)
    placed = placed[:side] + placed[side : 2 * side] + placed[2 * side :]
    for f in range(frames):
        for i in range(token_rows):
            at = f * token_rows + i
            out[pl.ds(at * side, side), :] = placed[:, at * cols : (at + 1) * cols]


def head_call(hidden, token_order, noisy, head_weight, head_mod, mean, std, w2, b2):
    tokens, width = hidden.shape[1:]
    outs = head_weight.shape[1]
    chans = w2.shape[0]
    frames, rows, row_lanes = noisy.shape
    cols = row_lanes // chans
    chunks = 5
    hbm = pl.BlockSpec(memory_space=pl.ANY)
    vmem = pltpu.VMEM
    return pl.pallas_call(
        head_kernel,
        out_shape=jax.ShapeDtypeStruct((frames * rows * (rows + 1) * chans, cols), F32),
        in_specs=[hbm] * 9,
        out_specs=pl.BlockSpec(memory_space=pltpu.VMEM),
        scratch_shapes=[
            vmem((tokens, width), BF16), vmem((outs, width), BF16), vmem((2, width), F32),
            vmem((1, tokens), jnp.int32), vmem(noisy.shape, F32),
            vmem((1, chans), F32), vmem((1, chans), F32), vmem(w2.shape, F32), vmem((1, chans), F32),
            vmem((2 * outs + 16, width), BF16), vmem((2 * tokens, 2 * tokens), BF16),
            vmem((frames * cols, 128), F32), vmem((tokens, 128), F32), vmem((tokens, 128), F32),
            pltpu.SemaphoreType.DMA((6,)), pltpu.SemaphoreType.DMA((2,)), pltpu.SemaphoreType.DMA((chunks,)),
        ],
        compiler_params=limit(20),
        name="head",
    )(
        *(
            pltpu.with_memory_space_constraint(value, pltpu.HBM)
            for value in (
                hidden.reshape(tokens, width), head_weight.T, head_mod, token_order.reshape(1, -1), noisy,
                mean.reshape(1, -1), std.reshape(1, -1), w2, b2.reshape(1, -1),
            )
        )
    )


def merge_kernel(frames, token_rows, by_half, mine, theirs, guide, step, table, own, edge):
    half = lax.axis_index("cfg")
    side = own.shape[0] // (frames * token_rows)
    chans = edge.shape[0] // frames
    tail = own.shape[0]
    gaps = iota(table.shape, 1) - step[0]
    gaps = jnp.where(gaps == 1, table[...], jnp.where(gaps == 0, -table[...], 0))
    delta = jnp.sum(gaps.astype(F32), axis=1, keepdims=True) * (1.0 / 1000.0)
    cond = guide[0] * delta
    uncond = delta - cond
    left = jnp.where(half == 0, cond, uncond)
    right = jnp.where(half == 0, uncond, cond)
    lower = half == 1 if by_half else lax.axis_index("rows") == 0
    for f in range(frames):
        spot = pl.ds(tail + f * side, side)
        near, far = mine[spot, :], theirs[spot, :]
        values = []
        for i in range(token_rows):
            at = pl.ds((f * token_rows + i) * side, side)
            value = left * mine[at, :] + right * theirs[at, :] + jnp.where(half == i, near, far)
            value = value.astype(BF16)
            own[at, :] = value
            values.append(value)
        edge[pl.ds(f * chans, chans), :] = jnp.where(lower, values[-1][side - chans :], values[0][:chans])


def merge_call(mine, theirs, guidance, index, table, frames, token_rows, chans, by_half):
    tall = frames * token_rows * token_rows * chans
    cols = mine.shape[1]
    vmem = pl.BlockSpec(memory_space=pltpu.VMEM)
    smem = pl.BlockSpec(memory_space=pltpu.SMEM)
    return pl.pallas_call(
        functools.partial(merge_kernel, frames, token_rows, by_half),
        out_shape=(
            jax.ShapeDtypeStruct((tall, cols), BF16),
            jax.ShapeDtypeStruct((frames * chans, cols), BF16),
        ),
        in_specs=[vmem, vmem, smem, smem, vmem],
        out_specs=(vmem, vmem),
        compiler_params=limit(4),
        name="merge",
    )(mine, theirs, guidance, index, table.reshape(1, -1))


def limit(mebibytes):
    return pltpu.CompilerParams(vmem_limit_bytes=mebibytes * 2**20)


def widen_kernel(rows, weight, after, early, late):
    _, chans, chans_out = weight.shape
    span = rows + 2
    for wide, base in ((early, 0), (late, 1)):
        for w in range(3):
            for t in range(2):
                for q in range(span):
                    at = pl.ds(((w * 2 + t) * span + q) * chans, chans)
                    for y in range(rows):
                        u = q - y
                        if 0 <= u < 3:
                            value = weight[9 * (t + base) + 3 * u + w]
                        else:
                            value = jnp.zeros((chans, chans_out), BF16)
                        wide[at, pl.ds(y * chans_out, chans_out)] = value


def widen_call(weight, after, rows):
    _, chans, chans_out = weight.shape
    vmem = pl.BlockSpec(memory_space=pltpu.VMEM)
    wide = jax.ShapeDtypeStruct((6 * (rows + 2) * chans, rows * chans_out), BF16)
    return pl.pallas_call(
        functools.partial(widen_kernel, rows),
        out_shape=(wide, wide),
        in_specs=[vmem, pl.BlockSpec(memory_space=pl.ANY)],
        out_specs=(vmem, vmem),
        compiler_params=limit(8),
        name="widen",
    )(weight, after)


def columns(stack_v):
    cols = stack_v.shape[1]
    picks = [iota((cols, cols), 0) + (w - 1) == iota((cols, cols), 1) for w in range(3)]
    pick = jnp.concatenate([jnp.where(hit, 1.0, 0.0).astype(BF16) for hit in picks], axis=0)
    moved = mm(pick, stack_v[...], NT).astype(BF16)
    depth = moved.shape[1] // 2
    sides = []
    for f in range(2):
        pieces = [moved[w * cols : (w + 1) * cols, f * depth : (f + 1) * depth] for w in range(3)]
        sides.append(jnp.concatenate(pieces, axis=1))
    return sides


def late_kernel(rows, own, near, wide, bias, total, stack_v):
    chans = near.shape[0] // 2
    band = own.shape[0] // 2
    row = lax.axis_index("rows")
    first = lax.axis_index("cfg") == 0
    inner = jnp.where(first, row > 0, row < lax.axis_size("rows") - 1)
    depth = stack_v.shape[0] // 4
    frames = []
    for f in range(2):
        edge = near[pl.ds(f * chans, chans), :]
        edge = jnp.where(inner, edge, jnp.zeros_like(edge))
        trim = band - (depth - chans)
        base = own[pl.ds(f * band, band), :]
        frames.append(
            jnp.where(
                first,
                jnp.concatenate([edge, base[: band - trim]], axis=0),
                jnp.concatenate([base[trim:], edge], axis=0),
            )
        )
    stack_v[0:depth, :] = jnp.zeros((depth, stack_v.shape[1]), BF16)
    stack_v[depth : 2 * depth, :] = frames[0]
    stack_v[2 * depth : 3 * depth, :] = frames[0]
    stack_v[3 * depth :, :] = frames[1]
    for f, side in enumerate(columns(stack_v)):
        total[f] = mm(side, wide[...]) + jnp.concatenate([bias[...]] * rows, axis=1)


def late_call(own, near, wide, bias, rows):
    cols = own.shape[1]
    depth = wide.shape[0] // 6
    vmem = pl.BlockSpec(memory_space=pltpu.VMEM)
    return pl.pallas_call(
        functools.partial(late_kernel, rows),
        out_shape=jax.ShapeDtypeStruct((2, cols, wide.shape[1]), F32),
        in_specs=[vmem] * 4,
        out_specs=vmem,
        scratch_shapes=[pltpu.VMEM((4 * depth, cols), BF16)],
        compiler_params=limit(8),
        name="late",
    )(own, near, wide, bias)


def early_kernel(prev, prev_near, wide, total, result, stack_v, out, out_sem):
    frames, rows, cols, chans_out = out.shape
    depth = stack_v.shape[0] // 4
    chans = depth // (rows + 2)
    band = 2 * rows * chans
    tail = prev.shape[0] - frames * chans
    row = lax.axis_index("rows")
    first = lax.axis_index("cfg") == 0
    past = lax.axis_index("seq") > 0
    inner = jnp.where(first, row > 0, row < lax.axis_size("rows") - 1)
    trim = band - (depth - chans)
    for f in range(frames):
        at = pl.ds(f * band, band)
        base = jnp.where(first, prev_near[at, :], prev[at, :])
        base = jnp.where(past, base, jnp.zeros_like(base))
        at = pl.ds(tail + f * chans, chans)
        edge = jnp.where(first, prev_near[at, :], prev[at, :])
        edge = jnp.where(past & inner, edge, jnp.zeros_like(edge))
        value = jnp.where(
            first,
            jnp.concatenate([edge, base[: band - trim]], axis=0),
            jnp.concatenate([base[trim:], edge], axis=0),
        )
        stack_v[f * depth : (f + 1) * depth, :] = value
        if f == 1:
            stack_v[2 * depth : 3 * depth, :] = value
    stack_v[3 * depth :, :] = jnp.zeros((depth, cols), BF16)
    stores = []
    for f, side in enumerate(columns(stack_v)):
        for y in range(rows):
            span = pl.ds(y * chans_out, chans_out)
            out[f, y] = (mm(side, wide[:, span]) + total[f, :, span]).astype(BF16)
            stores.append(pltpu.make_async_copy(out.at[f, y], result.at[f, y], out_sem.at[f * rows + y]))
            stores[-1].start()
    for copy in stores:
        copy.wait()


def early_call(prev, prev_near, wide, total, rows):
    frames, cols, _ = total.shape
    depth = wide.shape[0] // 6
    chans_out = wide.shape[1] // rows
    vmem = pl.BlockSpec(memory_space=pltpu.VMEM)
    return pl.pallas_call(
        early_kernel,
        out_shape=jax.ShapeDtypeStruct((frames, rows, cols, chans_out), BF16),
        in_specs=[vmem] * 4,
        out_specs=pl.BlockSpec(memory_space=pl.ANY),
        scratch_shapes=[
            pltpu.VMEM((4 * depth, cols), BF16),
            pltpu.VMEM((frames, rows, cols, chans_out), BF16),
            pltpu.SemaphoreType.DMA((frames * rows,)),
        ],
        compiler_params=limit(8),
        name="early",
    )(prev, prev_near, wide, total)


def routes(sizes, rule):
    seqs, rows, halves = sizes
    pairs = []
    for s in range(seqs):
        for r in range(rows):
            for c in range(halves):
                to = rule(s, r, c)
                if 0 <= to[0] < seqs and 0 <= to[1] < rows:
                    pairs.append(((s * rows + r) * halves + c, (to[0] * rows + to[1]) * halves + to[2]))
    return pairs


def send(value, sizes, rule):
    return lax.ppermute(value, RING, routes(sizes, rule))


def per_device(
    hidden,
    token_order,
    noisy_latent,
    head_weight,
    head_mod,
    guidance,
    timestep_index,
    step_table,
    vae_mean,
    vae_std,
    conv2_weight,
    conv2_bias,
    conv1_weight,
    conv1_bias,
):
    frames, rows, _ = noisy_latent.shape
    chans = conv2_weight.shape[0]
    sizes = tuple(lax.axis_size(axis) for axis in RING)
    seqs, row_count, _ = sizes
    part = head_call(
        hidden, token_order, noisy_latent, head_weight, head_mod, vae_mean, vae_std, conv2_weight, conv2_bias
    )
    other = send(part, sizes, lambda s, r, c: (s, r, 1 - c))
    own, edge = merge_call(
        part, other, guidance, timestep_index, step_table, frames, rows, chans, row_count != 2
    )
    if row_count == 2:
        top = seqs - 1

        def along(s, r, c):
            if c == 1:
                return (s + 1, r, 1) if s < top else (s, r, 0)
            return (s - 1, r, 0) if s > 0 else (s, r, 1)

        def across(s, r, c):
            if c == 1:
                return (s + 1, 1 - r, 1) if s < top else (s, 1 - r, 0)
            return (s - 1, r, 0) if s > 0 else (s, 1 - r, 1)

        prev = send(own, sizes, along)
        near = send(edge, sizes, lambda s, r, c: (s, 1 - r, c))
        prev_edge = send(edge, sizes, across)
        prev = jnp.concatenate([prev, near, prev_edge], axis=0)
        prev_near = send(prev, sizes, lambda s, r, c: (s, r, 1 - c))
    else:
        near = send(edge, sizes, lambda s, r, c: (s, r - 1, 1) if c == 0 else (s, r + 1, 0))
        prev = send(own, sizes, lambda s, r, c: (s + 1, r, c))
        prev_edge = send(edge, sizes, lambda s, r, c: (s + 1, r - 1, 1) if c == 0 else (s + 1, r + 1, 0))
        prev = prev_near = jnp.concatenate([prev, near, prev_edge], axis=0)
    early, late = widen_call(conv1_weight, edge, rows)
    total = late_call(own, near, late, conv1_bias.reshape(1, -1), rows)
    return early_call(prev, prev_near, early, total, rows)


def solution(mesh):
    return jax.shard_map(
        per_device,
        mesh=mesh,
        in_specs=(
            P("cfg", ("groups", "seq", "rows"), None),
            P(("groups", "seq", "rows")),
            P(("groups", "seq"), ("rows", "cfg"), None),
            P(),
            P(),
            P(),
            P(),
            P(),
            P(),
            P(),
            P(),
            P(),
            P(),
            P(),
        ),
        out_specs=P(("groups", "seq"), ("rows", "cfg"), None, None),
        check_vma=False,
    )
```

```python
import functools

import jax
import jax.numpy as jnp
from jax import lax
from jax.experimental import pallas as pl
from jax.experimental.pallas import tpu as pltpu
from jax.sharding import PartitionSpec as P


HIGHEST = lax.Precision.HIGHEST
F32 = jnp.float32
BF16 = jnp.bfloat16
NN = (((1,), (0,)), ((), ()))
NT = (((1,), (1,)), ((), ()))
TN = (((0,), (0,)), ((), ()))
RING = ("seq", "rows", "cfg")


def mm(left, right, dims=NN, precision=None):
    return lax.dot_general(left, right, dims, precision=precision, preferred_element_type=F32)


def iota(shape, dim):
    return lax.broadcasted_iota(jnp.int32, shape, dim)


def split(value, terms):
    parts = []
    for _ in range(terms):
        parts.append(value.astype(BF16))
        value = value - parts[-1].astype(F32)
    return parts


def head_kernel(
    hid, wt, mod, tok, noisy, mean, std, w2, b2,
    out,
    x_v, w_v, mod_v, tok_v, noisy_v, mean_v, std_v, w2_v, b2_v,
    wcat_v, place_v, mask_v, square_v, pivot_v, small_sem, w_sem, x_sem,
):
    tokens, width = x_v.shape
    outs = w_v.shape[0]
    chans = w2_v.shape[0]
    frames, token_rows, row_lanes = noisy_v.shape
    cols = row_lanes // chans
    cells = 2 * tokens
    chunks = x_sem.shape[0]
    chunk = width // chunks
    pairs = [
        (tok, tok_v), (w2, w2_v), (mean, mean_v), (std, std_v), (b2, b2_v), (noisy, noisy_v),
    ]
    small = [pltpu.make_async_copy(a, b, small_sem.at[i]) for i, (a, b) in enumerate(pairs)]
    big = [pltpu.make_async_copy(mod, mod_v, w_sem.at[0]), pltpu.make_async_copy(wt, w_v, w_sem.at[1])]
    loads = []
    for k in range(chunks):
        span = pl.ds(k * chunk, chunk)
        loads.append(pltpu.make_async_copy(hid.at[:, span], x_v.at[:, span], x_sem.at[k]))
    for copy in small + big + loads[:1]:
        copy.start()
    for copy in small:
        copy.wait()

    frame_cells = lax.axis_size("rows") * token_rows * (cols // 2)
    cell = tok_v[...] - lax.axis_index("seq") * frames * frame_cells
    late = jnp.zeros_like(cell)
    for f in range(1, frames):
        late = late + (cell >= f * frame_cells).astype(jnp.int32)
    local = (
        cell - late * frame_cells - lax.axis_index("rows") * token_rows * (cols // 2)
        + late * token_rows * (cols // 2)
    )
    block = 128
    for e in range(2):
        target = 2 * local + e
        for start in range(0, cells, block):
            hit = iota((block, tokens), 0) + start == target
            place_v[pl.ds(start, block), pl.ds(e * tokens, tokens)] = jnp.where(hit, 1.0, 0.0).astype(BF16)

    lanes = 128
    reps = lanes // chans
    spread = (iota((chans, lanes), 1) % chans == iota((chans, lanes), 0)).astype(F32)
    row8 = iota((8, chans), 0)
    stacked = jnp.where(row8 == 0, std_v[...], jnp.where(row8 == 1, mean_v[...], b2_v[...]))
    tiled = mm(stacked, spread, NN, HIGHEST)
    mix = mm(w2_v[...], spread, TN, HIGHEST)
    diag = jnp.where(iota((chans, lanes), 1) == iota((chans, lanes), 0), tiled[2:3], 0.0)
    offset = jnp.sum(
        jnp.where(iota((chans, lanes), 1) < chans, mix * tiled[1:2] + diag, 0.0), axis=1, keepdims=True
    )
    mix = mix * tiled[0:1]

    own = iota((reps, lanes), 1) // chans == iota((reps, lanes), 0)
    tail = frames * token_rows * token_rows * chans
    for a in range(token_rows):
        for f in range(frames):
            for j in range(row_lanes // lanes):
                piece = noisy_v[f, a : a + 1, j * lanes : (j + 1) * lanes]
                mask_v[pl.ds(f * cols + j * reps, reps), :] = jnp.where(own, piece, 0.0)
        noise = mm(mix, mask_v[...], NT, HIGHEST) + offset
        for f in range(frames):
            at = tail + (f * token_rows + a) * chans
            out[pl.ds(at, chans), :] = noise[:, f * cols : (f + 1) * cols]

    blocks = outs // chans
    spot_o = iota((outs, outs), 0) // chans
    spot_j = iota((outs, outs), 1) // chans
    match = (spot_o % 2 == spot_j // 2) & (spot_o // 2 == spot_j % 2)
    mixer = jnp.where(match, jnp.concatenate([mix[:, :outs]] * blocks, axis=0), 0.0)
    high, low = split(mixer, 2)
    mixer = jnp.concatenate([high, high, low], axis=1)

    for copy in big:
        copy.wait()
    for copy in loads[1:1]:
        copy.start()
    piece = 512
    col_sum = jnp.zeros((outs, lanes), F32)
    shift_sum = jnp.zeros((outs, lanes), F32)
    for start in range(0, width, piece):
        span = pl.ds(start, piece)
        weight = w_v[:, span].astype(F32)
        scaled = weight * (1.0 + mod_v[1:2, span])
        high = scaled.astype(BF16)
        wcat_v[0:outs, span] = high
        wcat_v[outs : 2 * outs, span] = (scaled - high.astype(F32)).astype(BF16)
        shifted = weight * mod_v[0:1, span]
        for j in range(0, piece, lanes):
            col_sum = col_sum + scaled[:, j : j + lanes]
            shift_sum = shift_sum + shifted[:, j : j + lanes]
    wcat_v[2 * outs :, :] = jnp.ones((wcat_v.shape[0] - 2 * outs, width), BF16)
    col_sum = jnp.sum(col_sum, axis=1, keepdims=True)
    shift_sum = jnp.sum(shift_sum, axis=1, keepdims=True)

    group = 16
    total = jnp.zeros((wcat_v.shape[0], tokens), F32)
    pivot_row = None
    for k in range(chunks):
        loads[k].wait()
        for copy in ():
            copy.start()
        span = pl.ds(k * chunk, chunk)
        for g in range(0, tokens, group):
            rows = pl.ds(g, group)
            values = x_v[rows, span].astype(F32)
            if k == 0:
                pivot = jnp.sum(values[:, :lanes], axis=1, keepdims=True) * (1.0 / lanes)
                pivot = jnp.broadcast_to(pivot, (group, lanes))
                pivot_v[rows, :] = pivot
                squares = jnp.zeros((group, lanes), F32)
            else:
                pivot = pivot_v[rows, :]
                squares = square_v[rows, :]
            for j in range(0, chunk, lanes):
                gap = values[:, j : j + lanes] - pivot
                squares = squares + gap * gap
            square_v[rows, :] = squares
        total = total + mm(wcat_v[:, span], x_v[:, span], NT)
        if k == 0:
            parts = jnp.concatenate(split(pivot_v[...], 3), axis=1)
            pivot_row = mm(jnp.ones((16, 3 * lanes), BF16), parts, NT)[0:1] * (1.0 / lanes)

    parts = jnp.concatenate(split(square_v[...], 3), axis=1)
    square = mm(jnp.ones((16, 3 * lanes), BF16), parts, NT)[0:1] * (1.0 / width)
    center = total[2 * outs : 2 * outs + 1] * (1.0 / width)
    gap = center - pivot_row
    inverse = lax.rsqrt(jnp.maximum(square - gap * gap, 0.0) + 1e-06)
    head = (total[0:outs] + total[outs : 2 * outs] - center * col_sum) * inverse + shift_sum
    high, low = split(head, 2)
    mixed = mm(mixer, jnp.concatenate([high, low, high], axis=0))
    side = outs // 2
    mixed = jnp.concatenate([mixed[:side], mixed[side:]], axis=1)
    placed = mm(jnp.concatenate(split(mixed, 3), axis=0), place_v[...], NT)
    placed = placed[:side] + placed[side : 2 * side] + placed[2 * side :]
    for f in range(frames):
        for i in range(token_rows):
            at = f * token_rows + i
            out[pl.ds(at * side, side), :] = placed[:, at * cols : (at + 1) * cols]


def head_call(hidden, token_order, noisy, head_weight, head_mod, mean, std, w2, b2):
    tokens, width = hidden.shape[1:]
    outs = head_weight.shape[1]
    chans = w2.shape[0]
    frames, rows, row_lanes = noisy.shape
    cols = row_lanes // chans
    chunks = 1
    hbm = pl.BlockSpec(memory_space=pl.ANY)
    vmem = pltpu.VMEM
    return pl.pallas_call(
        head_kernel,
        out_shape=jax.ShapeDtypeStruct((frames * rows * (rows + 1) * chans, cols), F32),
        in_specs=[hbm] * 9,
        out_specs=pl.BlockSpec(memory_space=pltpu.VMEM),
        scratch_shapes=[
            vmem((tokens, width), BF16), vmem((outs, width), BF16), vmem((2, width), F32),
            vmem((1, tokens), jnp.int32), vmem(noisy.shape, F32),
            vmem((1, chans), F32), vmem((1, chans), F32), vmem(w2.shape, F32), vmem((1, chans), F32),
            vmem((2 * outs + 16, width), BF16), vmem((2 * tokens, 2 * tokens), BF16),
            vmem((frames * cols, 128), F32), vmem((tokens, 128), F32), vmem((tokens, 128), F32),
            pltpu.SemaphoreType.DMA((6,)), pltpu.SemaphoreType.DMA((2,)), pltpu.SemaphoreType.DMA((chunks,)),
        ],
        compiler_params=limit(20),
        name="head",
    )(
        *(
            pltpu.with_memory_space_constraint(value, pltpu.HBM)
            for value in (
                hidden.reshape(tokens, width), head_weight.T, head_mod, token_order.reshape(1, -1), noisy,
                mean.reshape(1, -1), std.reshape(1, -1), w2, b2.reshape(1, -1),
            )
        )
    )


def merge_kernel(frames, token_rows, by_half, mine, theirs, guide, step, table, own, edge):
    half = lax.axis_index("cfg")
    side = own.shape[0] // (frames * token_rows)
    chans = edge.shape[0] // frames
    tail = own.shape[0]
    gaps = iota(table.shape, 1) - step[0]
    gaps = jnp.where(gaps == 1, table[...], jnp.where(gaps == 0, -table[...], 0))
    delta = jnp.sum(gaps.astype(F32), axis=1, keepdims=True) * (1.0 / 1000.0)
    cond = guide[0] * delta
    uncond = delta - cond
    left = jnp.where(half == 0, cond, uncond)
    right = jnp.where(half == 0, uncond, cond)
    lower = half == 1 if by_half else lax.axis_index("rows") == 0
    for f in range(frames):
        spot = pl.ds(tail + f * side, side)
        near, far = mine[spot, :], theirs[spot, :]
        values = []
        for i in range(token_rows):
            at = pl.ds((f * token_rows + i) * side, side)
            value = left * mine[at, :] + right * theirs[at, :] + jnp.where(half == i, near, far)
            value = value.astype(BF16)
            own[at, :] = value
            values.append(value)
        edge[pl.ds(f * chans, chans), :] = jnp.where(lower, values[-1][side - chans :], values[0][:chans])


def merge_call(mine, theirs, guidance, index, table, frames, token_rows, chans, by_half):
    tall = frames * token_rows * token_rows * chans
    cols = mine.shape[1]
    vmem = pl.BlockSpec(memory_space=pltpu.VMEM)
    smem = pl.BlockSpec(memory_space=pltpu.SMEM)
    return pl.pallas_call(
        functools.partial(merge_kernel, frames, token_rows, by_half),
        out_shape=(
            jax.ShapeDtypeStruct((tall, cols), BF16),
            jax.ShapeDtypeStruct((frames * chans, cols), BF16),
        ),
        in_specs=[vmem, vmem, smem, smem, vmem],
        out_specs=(vmem, vmem),
        compiler_params=limit(4),
        name="merge",
    )(mine, theirs, guidance, index, table.reshape(1, -1))


def limit(mebibytes):
    return pltpu.CompilerParams(vmem_limit_bytes=mebibytes * 2**20)


def widen_kernel(rows, weight, after, early, late):
    _, chans, chans_out = weight.shape
    span = rows + 2
    for wide, base in ((early, 0), (late, 1)):
        for w in range(3):
            for t in range(2):
                for q in range(span):
                    at = pl.ds(((w * 2 + t) * span + q) * chans, chans)
                    for y in range(rows):
                        u = q - y
                        if 0 <= u < 3:
                            value = weight[9 * (t + base) + 3 * u + w]
                        else:
                            value = jnp.zeros((chans, chans_out), BF16)
                        wide[at, pl.ds(y * chans_out, chans_out)] = value


def widen_call(weight, after, rows):
    _, chans, chans_out = weight.shape
    vmem = pl.BlockSpec(memory_space=pltpu.VMEM)
    wide = jax.ShapeDtypeStruct((6 * (rows + 2) * chans, rows * chans_out), BF16)
    return pl.pallas_call(
        functools.partial(widen_kernel, rows),
        out_shape=(wide, wide),
        in_specs=[vmem, pl.BlockSpec(memory_space=pl.ANY)],
        out_specs=(vmem, vmem),
        compiler_params=limit(8),
        name="widen",
    )(weight, after)


def columns(stack_v):
    cols = stack_v.shape[1]
    picks = [iota((cols, cols), 0) + (w - 1) == iota((cols, cols), 1) for w in range(3)]
    pick = jnp.concatenate([jnp.where(hit, 1.0, 0.0).astype(BF16) for hit in picks], axis=0)
    moved = mm(pick, stack_v[...], NT).astype(BF16)
    depth = moved.shape[1] // 2
    sides = []
    for f in range(2):
        pieces = [moved[w * cols : (w + 1) * cols, f * depth : (f + 1) * depth] for w in range(3)]
        sides.append(jnp.concatenate(pieces, axis=1))
    return sides


def late_kernel(rows, own, near, wide, bias, total, stack_v):
    chans = near.shape[0] // 2
    band = own.shape[0] // 2
    row = lax.axis_index("rows")
    first = lax.axis_index("cfg") == 0
    inner = jnp.where(first, row > 0, row < lax.axis_size("rows") - 1)
    depth = stack_v.shape[0] // 4
    frames = []
    for f in range(2):
        edge = near[pl.ds(f * chans, chans), :]
        edge = jnp.where(inner, edge, jnp.zeros_like(edge))
        trim = band - (depth - chans)
        base = own[pl.ds(f * band, band), :]
        frames.append(
            jnp.where(
                first,
                jnp.concatenate([edge, base[: band - trim]], axis=0),
                jnp.concatenate([base[trim:], edge], axis=0),
            )
        )
    stack_v[0:depth, :] = jnp.zeros((depth, stack_v.shape[1]), BF16)
    stack_v[depth : 2 * depth, :] = frames[0]
    stack_v[2 * depth : 3 * depth, :] = frames[0]
    stack_v[3 * depth :, :] = frames[1]
    for f, side in enumerate(columns(stack_v)):
        total[f] = mm(side, wide[...]) + jnp.concatenate([bias[...]] * rows, axis=1)


def late_call(own, near, wide, bias, rows):
    cols = own.shape[1]
    depth = wide.shape[0] // 6
    vmem = pl.BlockSpec(memory_space=pltpu.VMEM)
    return pl.pallas_call(
        functools.partial(late_kernel, rows),
        out_shape=jax.ShapeDtypeStruct((2, cols, wide.shape[1]), F32),
        in_specs=[vmem] * 4,
        out_specs=vmem,
        scratch_shapes=[pltpu.VMEM((4 * depth, cols), BF16)],
        compiler_params=limit(8),
        name="late",
    )(own, near, wide, bias)


def early_kernel(prev, prev_near, wide, total, result, stack_v, out, out_sem):
    frames, rows, cols, chans_out = out.shape
    depth = stack_v.shape[0] // 4
    chans = depth // (rows + 2)
    band = 2 * rows * chans
    tail = prev.shape[0] - frames * chans
    row = lax.axis_index("rows")
    first = lax.axis_index("cfg") == 0
    past = lax.axis_index("seq") > 0
    inner = jnp.where(first, row > 0, row < lax.axis_size("rows") - 1)
    trim = band - (depth - chans)
    for f in range(frames):
        at = pl.ds(f * band, band)
        base = jnp.where(first, prev_near[at, :], prev[at, :])
        base = jnp.where(past, base, jnp.zeros_like(base))
        at = pl.ds(tail + f * chans, chans)
        edge = jnp.where(first, prev_near[at, :], prev[at, :])
        edge = jnp.where(past & inner, edge, jnp.zeros_like(edge))
        value = jnp.where(
            first,
            jnp.concatenate([edge, base[: band - trim]], axis=0),
            jnp.concatenate([base[trim:], edge], axis=0),
        )
        stack_v[f * depth : (f + 1) * depth, :] = value
        if f == 1:
            stack_v[2 * depth : 3 * depth, :] = value
    stack_v[3 * depth :, :] = jnp.zeros((depth, cols), BF16)
    stores = []
    for f, side in enumerate(columns(stack_v)):
        for y in range(rows):
            span = pl.ds(y * chans_out, chans_out)
            out[f, y] = (mm(side, wide[:, span]) + total[f, :, span]).astype(BF16)
            stores.append(pltpu.make_async_copy(out.at[f, y], result.at[f, y], out_sem.at[f * rows + y]))
            stores[-1].start()
    for copy in stores:
        copy.wait()


def early_call(prev, prev_near, wide, total, rows):
    frames, cols, _ = total.shape
    depth = wide.shape[0] // 6
    chans_out = wide.shape[1] // rows
    vmem = pl.BlockSpec(memory_space=pltpu.VMEM)
    return pl.pallas_call(
        early_kernel,
        out_shape=jax.ShapeDtypeStruct((frames, rows, cols, chans_out), BF16),
        in_specs=[vmem] * 4,
        out_specs=pl.BlockSpec(memory_space=pl.ANY),
        scratch_shapes=[
            pltpu.VMEM((4 * depth, cols), BF16),
            pltpu.VMEM((frames, rows, cols, chans_out), BF16),
            pltpu.SemaphoreType.DMA((frames * rows,)),
        ],
        compiler_params=limit(8),
        name="early",
    )(prev, prev_near, wide, total)


def routes(sizes, rule):
    seqs, rows, halves = sizes
    pairs = []
    for s in range(seqs):
        for r in range(rows):
            for c in range(halves):
                to = rule(s, r, c)
                if 0 <= to[0] < seqs and 0 <= to[1] < rows:
                    pairs.append(((s * rows + r) * halves + c, (to[0] * rows + to[1]) * halves + to[2]))
    return pairs


def send(value, sizes, rule):
    return lax.ppermute(value, RING, routes(sizes, rule))


def per_device(
    hidden,
    token_order,
    noisy_latent,
    head_weight,
    head_mod,
    guidance,
    timestep_index,
    step_table,
    vae_mean,
    vae_std,
    conv2_weight,
    conv2_bias,
    conv1_weight,
    conv1_bias,
):
    frames, rows, _ = noisy_latent.shape
    chans = conv2_weight.shape[0]
    sizes = tuple(lax.axis_size(axis) for axis in RING)
    seqs, row_count, _ = sizes
    part = head_call(
        hidden, token_order, noisy_latent, head_weight, head_mod, vae_mean, vae_std, conv2_weight, conv2_bias
    )
    other = send(part, sizes, lambda s, r, c: (s, r, 1 - c))
    own, edge = merge_call(
        part, other, guidance, timestep_index, step_table, frames, rows, chans, row_count != 2
    )
    if row_count == 2:
        top = seqs - 1

        def along(s, r, c):
            if c == 1:
                return (s + 1, r, 1) if s < top else (s, r, 0)
            return (s - 1, r, 0) if s > 0 else (s, r, 1)

        def across(s, r, c):
            if c == 1:
                return (s + 1, 1 - r, 1) if s < top else (s, 1 - r, 0)
            return (s - 1, r, 0) if s > 0 else (s, 1 - r, 1)

        prev = send(own, sizes, along)
        near = send(edge, sizes, lambda s, r, c: (s, 1 - r, c))
        prev_edge = send(edge, sizes, across)
        prev = jnp.concatenate([prev, near, prev_edge], axis=0)
        prev_near = send(prev, sizes, lambda s, r, c: (s, r, 1 - c))
    else:
        near = send(edge, sizes, lambda s, r, c: (s, r - 1, 1) if c == 0 else (s, r + 1, 0))
        prev = send(own, sizes, lambda s, r, c: (s + 1, r, c))
        prev_edge = send(edge, sizes, lambda s, r, c: (s + 1, r - 1, 1) if c == 0 else (s + 1, r + 1, 0))
        prev = prev_near = jnp.concatenate([prev, near, prev_edge], axis=0)
    early, late = widen_call(conv1_weight, edge, rows)
    total = late_call(own, near, late, conv1_bias.reshape(1, -1), rows)
    return early_call(prev, prev_near, early, total, rows)


def solution(mesh):
    return jax.shard_map(
        per_device,
        mesh=mesh,
        in_specs=(
            P("cfg", ("groups", "seq", "rows"), None),
            P(("groups", "seq", "rows")),
            P(("groups", "seq"), ("rows", "cfg"), None),
            P(),
            P(),
            P(),
            P(),
            P(),
            P(),
            P(),
            P(),
            P(),
            P(),
            P(),
        ),
        out_specs=P(("groups", "seq"), ("rows", "cfg"), None, None),
        check_vma=False,
    )
```
